32 devices in a mesh: replica: 4 (over x, core), fsdp: 8 (over z, y).
Axes of the slice: x: 2, y: 2, z: 4, core: 2. Of those that a mesh axis runs over, the one named last changes fastest.
Arguments:
- byte_input: bfloat16 [32768, 768], P(('replica', 'fsdp')), may hold values from -6 to 6
- global_out: bfloat16 [32768, 768], P(('replica', 'fsdp')), may hold values from -6 to 6
- cotangent: bfloat16 [32768, 768], P(('replica', 'fsdp')), may hold values from -6 to 6
- seq_patches: int32 [4, 4], P('replica'), may hold values from 1 to 512, 1024 in all within a row
- last_fill: int32 [4, 4], P('replica'), may hold values from 1 to 8
- deal_slots: int32 [4, 1024], P('replica', 'fsdp'), may hold values from 0 to 1023, as said below
- first_gain: bfloat16 [768], P('fsdp'), may hold values from 0.5 to 1.5
- first_shift: bfloat16 [768], P('fsdp'), may hold values from -1.796875 to 1.796875
- qkv_weight: bfloat16 [768, 2304], P('fsdp'), may hold values from -0.21875 to 0.21875
- out_weight: bfloat16 [768, 768], P('fsdp'), may hold values from -0.4375 to 0.4375
- second_gain: bfloat16 [768], P('fsdp'), may hold values from 0.5 to 1.5
- second_shift: bfloat16 [768], P('fsdp'), may hold values from -1.796875 to 1.796875
- up_weight: bfloat16 [768, 3072], P('fsdp'), may hold values from -0.21875 to 0.21875
- up_bias: bfloat16 [3072], P('fsdp'), may hold values from -3 to 3
- down_weight: bfloat16 [3072, 768], P('fsdp'), may hold values from -0.15625 to 0.15625
- down_bias: bfloat16 [768], P('fsdp'), may hold values from -1.796875 to 1.796875
Outputs:
- layer_out: bfloat16 [32768, 768], P(('replica', 'fsdp'))
- grad_input: bfloat16 [32768, 768], P(('replica', 'fsdp'))
- grad_global: bfloat16 [32768, 768], P(('replica', 'fsdp'))
- grad_first_gain: float32 [768], P('fsdp')
- grad_first_shift: float32 [768], P('fsdp')
- grad_qkv_weight: float32 [768, 2304], P('fsdp')
- grad_out_weight: float32 [768, 768], P('fsdp')
- grad_second_gain: float32 [768], P('fsdp')
- grad_second_shift: float32 [768], P('fsdp')
- grad_up_weight: float32 [768, 3072], P('fsdp')
- grad_up_bias: float32 [3072], P('fsdp')
- grad_down_weight: float32 [3072, 768], P('fsdp')
- grad_down_bias: float32 [768], P('fsdp')
The draws below stay inside these ranges and needn't reach their ends.
Inputs may be any that keep to these rules, and one draw needn't show every extreme that they name: `seq_patches`: row g gives the patches of the 4 sequences of group g in order; each row sums to 1024 and its largest entry is 512. `last_fill`: bytes used in the last patch of each sequence; the rest of that patch is padding. Each row is a permutation of 0 to 1023. Of the patches p in any aligned block of 128, exactly 16 have deal_slots in each aligned block of 128 positions.
All inputs are finite; a program needn't handle non-finite values.
Results may differ from the reference program's by a relative error of at most 0.017.
Values may be sent and summed in bfloat16 or wider, within the bound.
No kernel may reach another device: no remote copies, remote signals or barrier semaphores. Data moves between devices by JAX's collectives and lax.ppermute only.
A program may use at most 128 MiB of HBM per device.

```python
import math
import jax
import jax.numpy as jnp
import numpy as np
from jax import lax

D = 768
HEADS = 12
HEAD_DIM = 64
FF = 3072
PATCH = 8
SEQS = 4
PATCH_DEV = 128
GROUP_PATCHES = 1024
MOST_PATCHES = 512
DEAL_SHARE = 16
TOKENS = 32768
N_REPLICA = 4
N_FSDP = 8


def draw_deal_slots(key, part):
    base_ids = jnp.arange(PATCH_DEV, dtype=jnp.int32)

    def one_group(group_key):
        source_key, target_key = jax.random.split(jax.random.fold_in(group_key, 11))
        source_perm = jax.vmap(lambda k: jax.random.permutation(k, base_ids))(jax.random.split(source_key, N_FSDP))
        target_perm = jax.vmap(lambda k: jax.random.permutation(k, base_ids))(jax.random.split(target_key, N_FSDP))
        target = source_perm // DEAL_SHARE
        within = source_perm % DEAL_SHARE
        source = jnp.arange(N_FSDP, dtype=jnp.int32)[:, None]
        dealt = target_perm[target, source * DEAL_SHARE + within]
        return (target * PATCH_DEV + dealt).reshape(GROUP_PATCHES)
    return jax.vmap(one_group)(jax.random.split(key, N_REPLICA)).astype(jnp.int32)


def place_ends(array, key, smallest, top_value):
    place = [jax.random.randint(jax.random.fold_in(key, axis), (), 0, length) for axis, length in enumerate(array.shape)]
    widest = array.shape.index(max(array.shape))
    next_to = place[:widest] + [(place[widest] + 1) % array.shape[widest]] + place[widest + 1:]
    return array.at[tuple(place)].set(smallest).at[tuple(next_to)].set(top_value)


def steps_of(stream_key, shape, cuts, smallest, largest):
    factor_of = 1.0
    for position, shards_of in cuts:
        heights = jax.random.uniform(jax.random.fold_in(jax.random.fold_in(stream_key, 6), position), (shards_of,), jnp.float32, smallest / len(cuts), largest / len(cuts))
        factor_of = factor_of * jnp.repeat(jnp.exp(heights), shape[position] // shards_of).reshape((-1,) + (1,) * (len(shape) - 1 - position))
    return factor_of


def length_profile(amount, total, most, lean):
    weights = [(1 << 20) // math.isqrt(standing ** lean) + 1 for standing in range(2, amount + 1)]
    spare, given = total - most - (amount - 1), [1] * (amount - 1)
    while spare > 0:
        free = [i for i in range(amount - 1) if given[i] < most]
        mass, remaining = sum([weights[i] for i in free]), spare
        for i in free:
            addition = min(most - given[i], max(1, remaining * weights[i] // mass), spare)
            given[i] = given[i] + addition
            spare = spare - addition
    return np.array([most] + given)


def ragged_sizes(stream_key, count, total, most, slope):
    if count == 2:
        one = jax.random.randint(stream_key, (), max(1, total - most), min(most, total - 1) + 1)
        return jnp.stack([one, total - one])
    sizes = jnp.asarray(length_profile(count, total, most, slope), jnp.int32)
    couples = (count - 1) // 2
    donor, taker = sizes[1:1 + 2 * couples:2], sizes[2:2 + 2 * couples:2]
    room = jnp.minimum(donor - 1, most - taker)
    moved = jax.random.randint(jax.random.fold_in(stream_key, 1), (couples,), 0, 1 << 20) % (room + 1)
    sizes = sizes.at[1:1 + 2 * couples:2].set(donor - moved).at[2:2 + 2 * couples:2].set(taker + moved)
    return sizes[jax.random.permutation(jax.random.fold_in(stream_key, 2), count)]


def scatter_about(key, extent, width, reach, cuts=(), kind=jnp.bfloat16):
    loudness = steps_of(key, extent, cuts, -0.22, 0.18) if cuts else 1.0
    array = jax.random.normal(key, extent, jnp.float32) * width * loudness
    return jnp.minimum(jnp.maximum(array, -reach), reach).astype(kind)


def setup_inputs(seed: int = 0) -> dict:
    streams_of = jax.random.split(jax.random.key(seed), 17)
    byte_input = scatter_about(streams_of[0], (TOKENS, D), 1.0, 6.0, ((0, 32),))
    global_out = scatter_about(streams_of[1], (TOKENS, D), 1.0, 6.0, ((0, 32),))
    cotangent = scatter_about(streams_of[2], (TOKENS, D), 1.0, 6.0, ((0, 32),))
    seq_patches = jax.vmap(lambda own: ragged_sizes(own, SEQS, GROUP_PATCHES, MOST_PATCHES, 1))(jax.random.split(streams_of[3], N_REPLICA)).reshape((N_REPLICA, SEQS)).astype(jnp.int32)
    last_fill = place_ends(jax.random.randint(streams_of[4], (N_REPLICA, SEQS), 1, PATCH + 1), jax.random.fold_in(streams_of[4], 1), 1, PATCH).astype(jnp.int32)
    deal_slots = draw_deal_slots(jax.random.fold_in(streams_of[16], 71), 0)
    first_gain = jnp.clip(1.0 + 0.1 * jax.random.normal(streams_of[6], (D,), jnp.float32), 0.5, 1.5).astype(jnp.bfloat16)
    first_shift = scatter_about(streams_of[7], (D,), 0.3, 1.796875, ((0, 8),))
    qkv_weight = scatter_about(streams_of[8], (D, 3 * D), D ** -0.5, 0.21875, ((0, 8),))
    out_weight = scatter_about(streams_of[9], (D, D), (D // 4) ** -0.5, 0.4375, ((0, 8),))
    second_gain = jnp.clip(1.0 + 0.1 * jax.random.normal(streams_of[10], (D,), jnp.float32), 0.5, 1.5).astype(jnp.bfloat16)
    second_shift = scatter_about(streams_of[11], (D,), 0.3, 1.796875, ((0, 8),))
    up_weight = scatter_about(streams_of[12], (D, FF), D ** -0.5, 0.21875, ((0, 8),))
    up_bias = scatter_about(streams_of[13], (FF,), 0.5, 3.0, ((0, 8),))
    down_weight = scatter_about(streams_of[14], (FF, D), (FF // 2) ** -0.5, 0.15625, ((0, 8),))
    down_bias = scatter_about(streams_of[15], (D,), 0.3, 1.796875, ((0, 8),))
    return dict(byte_input=byte_input, global_out=global_out, cotangent=cotangent, seq_patches=seq_patches, last_fill=last_fill, deal_slots=deal_slots, first_gain=first_gain, first_shift=first_shift, qkv_weight=qkv_weight, out_weight=out_weight, second_gain=second_gain, second_shift=second_shift, up_weight=up_weight, up_bias=up_bias, down_weight=down_weight, down_bias=down_bias)


@jax.custom_vjp
def low(v):
    return lax.optimization_barrier(v.astype(jnp.bfloat16)).astype(jnp.float32)

@jax.custom_vjp
def low_back(v):
    return v

def low_keep(v):
    return (low(v), None)

def low_pass(kept, grad):
    return (grad,)

def back_keep(v):
    return (v, None)

def back_low(kept, grad):
    return (low(grad),)
low.defvjp(low_keep, low_pass)
low_back.defvjp(back_keep, back_low)
EPSILON = 1e-05

def product(left, right):
    return jnp.dot(left, right, precision=lax.Precision.HIGHEST, preferred_element_type=jnp.float32)

def normalize(values, gain, shift):
    center = values - lax.optimization_barrier(jnp.mean(values, axis=1, keepdims=True))
    inverse = lax.rsqrt(lax.optimization_barrier(jnp.mean(jnp.square(center), axis=1, keepdims=True)) + EPSILON)
    return center * inverse * gain + shift

def block_layer(residual_input, keep_rows, params):
    first_gain, first_shift, qkv_weight, out_weight, second_gain, second_shift, up_weight, up_bias, down_weight, down_bias = params
    row_count = residual_input.shape[0]
    model_width = residual_input.shape[1]
    first_in = low(normalize(residual_input, first_gain, first_shift))
    qkv_rows = low_back(low(product(first_in, qkv_weight)))
    patches = row_count // PATCH
    queries = qkv_rows[:, :model_width].reshape(patches, PATCH, HEADS, HEAD_DIM)
    keys_part = qkv_rows[:, model_width:2 * model_width].reshape(patches, PATCH, HEADS, HEAD_DIM)
    values_part = qkv_rows[:, 2 * model_width:].reshape(patches, PATCH, HEADS, HEAD_DIM)
    scores = jnp.einsum('pqhd,pkhd->phqk', queries, keys_part, precision=lax.Precision.HIGHEST) * HEAD_DIM ** (-0.5)
    scores = low_back(scores)
    causal = jnp.tril(jnp.ones((PATCH, PATCH), dtype=bool))
    scores = jnp.where(causal, scores, -1e+30)
    probs = low(jax.nn.softmax(scores, axis=-1))
    mixed = jnp.einsum('phqk,pkhd->pqhd', probs, values_part, precision=lax.Precision.HIGHEST)
    attended = low_back(low(mixed.reshape(row_count, model_width)))
    residual_midway = residual_input + low_back(product(attended, out_weight))
    second_in = low(normalize(residual_midway, second_gain, second_shift))
    pre_act = low_back(product(second_in, up_weight) + up_bias)
    activ = low(jax.nn.gelu(pre_act, approximate=False))
    result = residual_midway + product(activ, down_weight) + down_bias
    return keep_rows * result

def reference(byte_input, global_out, cotangent, seq_patches, last_fill, deal_slots, first_gain, first_shift, qkv_weight, out_weight, second_gain, second_shift, up_weight, up_bias, down_weight, down_bias):
    groups = seq_patches.shape[0]
    group_patches = deal_slots.shape[1]
    model_width = byte_input.shape[1]
    patch_ids = jnp.arange(group_patches, dtype=jnp.int32)
    seq_ends = jnp.cumsum(seq_patches, axis=1).astype(jnp.int32)
    seq_ids = lax.optimization_barrier(jnp.sum((patch_ids[None, :, None] >= seq_ends[:, None, :]).astype(jnp.int32), axis=2)).astype(jnp.int32)
    end_of = jnp.take_along_axis(seq_ends, seq_ids, axis=1)
    fill_of = jnp.take_along_axis(last_fill, seq_ids, axis=1)
    in_patch = jnp.arange(PATCH, dtype=jnp.int32)
    keep_byte = (patch_ids[None, :] != end_of - 1)[:, :, None] | (in_patch[None, None, :] < fill_of[:, :, None])
    keep_rows = keep_byte.astype(jnp.float32).reshape(TOKENS, 1)
    block_rows = math.gcd(TOKENS, 4096)
    block_count = TOKENS // block_rows
    group_index = jnp.arange(groups, dtype=jnp.int32)[:, None]
    stepper = jax.checkpoint(block_layer)

    def forward(inputs, dealt, params):
        arranged = dealt.reshape(groups, group_patches, PATCH, model_width)[group_index, deal_slots]
        residual_input = inputs + arranged.reshape(TOKENS, model_width)
        outputs = lax.map(lambda pair: stepper(pair[0], pair[1], params), (residual_input.reshape(block_count, block_rows, model_width), keep_rows.reshape(block_count, block_rows, 1)))
        return outputs.reshape(TOKENS, model_width)
    weights = (first_gain.astype(jnp.float32), first_shift.astype(jnp.float32), qkv_weight.astype(jnp.float32), out_weight.astype(jnp.float32), second_gain.astype(jnp.float32), second_shift.astype(jnp.float32), up_weight.astype(jnp.float32), up_bias.astype(jnp.float32), down_weight.astype(jnp.float32), down_bias.astype(jnp.float32))
    layer_out, pullback = jax.vjp(forward, byte_input.astype(jnp.float32), global_out.astype(jnp.float32), weights)
    grad_input, grad_global, grads = pullback(cotangent.astype(jnp.float32))
    return (layer_out.astype(jnp.bfloat16), grad_input.astype(jnp.bfloat16), grad_global.astype(jnp.bfloat16), grads[0], grads[1], grads[2], grads[3], grads[4], grads[5], grads[6], grads[7], grads[8], grads[9])
```

```python
import jax
import jax.numpy as jnp
from jax import lax
from jax.sharding import PartitionSpec as P

HEADS = 12
HEAD_DIM = 64
PATCH = 8
EPSILON = 1e-05
BF16 = jnp.bfloat16
F32 = jnp.float32


def contract_rows(left, right):
    return lax.dot_general(left, right, (((0,), (0,)), ((), ())), preferred_element_type=F32)


def contract_cols(left, right):
    return lax.dot_general(left, right, (((1,), (1,)), ((), ())), preferred_element_type=F32)


def apply_layer_normalize(values, gain, shift):
    center = values - jnp.mean(values, axis=1, keepdims=True)
    inverse = lax.rsqrt(jnp.mean(jnp.square(center), axis=1, keepdims=True) + EPSILON)
    normed = center * inverse
    return (normed * gain + shift, normed, inverse)


def normalize_pullback(upstream, gain, normed, inverse):
    scaled = upstream * gain
    inner = (
        scaled
        - jnp.mean(scaled, axis=1, keepdims=True)
        - normed * jnp.mean(scaled * normed, axis=1, keepdims=True)
    )
    return (inverse * inner, jnp.sum(upstream * normed, axis=0), jnp.sum(upstream, axis=0))


def block_mask(span):
    index = jnp.arange(span, dtype=jnp.int32)
    return (index[:, None] // PATCH == index[None, :] // PATCH) & (index[None, :] <= index[:, None])


def attention_scores(queries, keys_part, allowed):
    raw = jnp.einsum(
        "gqhd,gkhd->ghqk", queries, keys_part, preferred_element_type=F32
    ) * HEAD_DIM ** (-0.5)
    return jnp.where(allowed, raw, -1e30)


class Links:
    def __init__(self, n_replica, n_fsdp, shard_rows):
        self.n = {"replica": n_replica, "fsdp": n_fsdp}
        self.at = {"replica": lax.axis_index("replica"), "fsdp": lax.axis_index("fsdp")}
        split = n_replica
        while (shard_rows // split) % 8 or shard_rows % split:
            split //= 2
        self.split = split
        y_count = min(max(n_replica // 2, 1), n_fsdp)

        def bits(low, high):
            found = []
            while low < high:
                found.append(low)
                low *= 2
            return found

        self.core = [("replica", b) for b in bits(1, min(2, split))]
        self.x = [("replica", b) for b in bits(2, split)]
        self.rest = [("replica", b) for b in bits(split, n_replica)]
        self.y = [("fsdp", b) for b in bits(1, y_count)]
        self.z = [("fsdp", b) for b in bits(y_count, n_fsdp)]
        self.quarter = self.at["replica"] % split

    def swap(self, values, step):
        axis, mask = step
        return lax.ppermute(values, axis, [(i, i ^ mask) for i in range(self.n[axis])])

    def my_bit(self, step):
        axis, mask = step
        return (self.at[axis] // mask) % 2

    def gather(self, piece, steps):
        for step in steps:
            piece = jnp.concatenate([piece, self.swap(piece, step)], axis=0)
        return piece

    def place_of(self, steps):
        shards = jnp.arange(self.n["fsdp"], dtype=jnp.int32)[:, None]
        quarters = jnp.arange(self.split, dtype=jnp.int32)[None, :]
        apart = {"fsdp": shards ^ self.at["fsdp"], "replica": quarters ^ self.quarter}
        place = jnp.zeros((self.n["fsdp"], self.split), jnp.int32)
        for position, (axis, mask) in enumerate(steps):
            place = place + ((apart[axis] // mask) % 2) * (1 << position)
        return place.reshape(-1)

    def reduce(self, values, steps):
        axes = list(reversed(self.z)) + list(reversed(self.y)) + list(reversed(self.x)) + self.core
        rest = values.shape[2:]
        values = values.reshape((2,) * len(axes) + rest)
        for step in steps:
            dim = axes.index(step)
            mine = self.my_bit(step)
            keep = lax.dynamic_index_in_dim(values, mine, dim, keepdims=False)
            send = lax.dynamic_index_in_dim(values, 1 - mine, dim, keepdims=False)
            got = self.swap(send, step)
            values = (keep.astype(F32) + got.astype(F32)).astype(BF16)
            axes.remove(step)
        for step in self.rest:
            values = (values.astype(F32) + self.swap(values, step).astype(F32)).astype(BF16)
        return values.reshape(rest)


def body(
    byte_input,
    global_out,
    cotangent,
    seq_patches,
    last_fill,
    deal_slots,
    first_gain,
    first_shift,
    qkv_weight,
    out_weight,
    second_gain,
    second_shift,
    up_weight,
    up_bias,
    down_weight,
    down_bias,
):
    row_count = byte_input.shape[0]
    model_width = byte_input.shape[1]
    patch_count = row_count // PATCH
    fsdp_count = lax.axis_size("fsdp")
    replica_count = lax.axis_size("replica")
    share = patch_count // fsdp_count
    shard = qkv_weight.shape[0]
    links = Links(replica_count, fsdp_count, shard)
    split = links.split
    part = shard // split
    down_part = down_weight.shape[0] // split
    ff = up_weight.shape[1]
    blocks_up = ff // model_width

    target = deal_slots[0] // patch_count
    dealt_slot = deal_slots[0] % patch_count
    dest_hits = (target[:, None] == jnp.arange(fsdp_count, dtype=jnp.int32)[None, :]).astype(jnp.int32)
    dest_rank = jnp.sum((jnp.cumsum(dest_hits, axis=0) - 1) * dest_hits, axis=1)
    send_place = target * share + dest_rank
    send_order = (
        jnp.zeros((patch_count,), jnp.int32)
        .at[send_place]
        .set(jnp.arange(patch_count, dtype=jnp.int32))
    )
    wanted_slot = lax.all_to_all(
        dealt_slot[send_order], "fsdp", split_axis=0, concat_axis=0, tiled=True
    )

    def pick(values, order):
        return values.reshape(patch_count, PATCH, model_width)[order].reshape(row_count, model_width)

    arrived = lax.all_to_all(
        pick(global_out, wanted_slot), "fsdp", split_axis=0, concat_axis=0, tiled=True
    )

    def my_part(values, size):
        return lax.dynamic_slice_in_dim(values, links.quarter * size, size, axis=0)

    def cut(values):
        return [
            lax.slice_in_dim(values, i * model_width, (i + 1) * model_width, axis=1)
            for i in range(values.shape[1] // model_width)
        ]

    small = jnp.concatenate([first_gain, first_shift, second_gain, second_shift, down_bias])
    small = jnp.pad(small, (0, model_width - small.shape[0]))
    bias_row = jnp.pad(up_bias, (0, model_width - up_bias.shape[0]))
    vectors = jnp.pad(jnp.stack([small, bias_row]), ((0, 6), (0, 0)))

    qkv_mine = my_part(qkv_weight, part)
    out_mine = my_part(out_weight, part)
    up_mine = my_part(up_weight, part)
    down_mine = my_part(down_weight, down_part)
    q_mine, k_mine, v_mine = cut(qkv_mine)
    first_piece = jnp.concatenate([vectors, q_mine, k_mine, v_mine, out_mine], axis=0)
    second_piece = jnp.concatenate(cut(up_mine), axis=0)
    third_piece = down_mine

    z_steps = list(reversed(links.z))
    order_a = links.y + links.x + links.core
    order_b = links.x + links.y + links.core
    place_a = links.place_of(z_steps + order_a)
    place_b = links.place_of(z_steps + order_b)

    def gather_group(piece, at):
        rows = piece.shape[0]
        got = links.gather(piece[None], z_steps)
        a = links.gather(got[:, :at], order_a)
        b = links.gather(got[:, at:], order_b)
        a = a[place_a].reshape(fsdp_count, split, at, model_width)
        b = b[place_b].reshape(fsdp_count, split, rows - at, model_width)
        return a, b

    def block_of(values, start):
        return lax.slice_in_dim(values, start, start + part, axis=2).reshape(model_width, model_width)

    g1a, g1b = gather_group(first_piece, 8 + 2 * part)
    vec = g1a[:, 0, :8]
    widths = [0, 1, 2, 3, 4]
    gain_full, shift_full, gain_later, shift_later, reduce_bias = [
        vec[:, 0, i * shard : (i + 1) * shard].reshape(model_width).astype(F32) for i in widths
    ]
    expand_bias = vec[:, 1, : up_bias.shape[0]].reshape(ff).astype(F32)
    qkv_full = jnp.concatenate(
        [block_of(g1a, 8), block_of(g1a, 8 + part), block_of(g1b, 0)], axis=1
    )
    outproj_full = block_of(g1b, part)
    half_up = blocks_up // 2
    g2a, g2b = gather_group(second_piece, half_up * part)
    expand_full = jnp.concatenate(
        [block_of(g2a, i * part) for i in range(half_up)]
        + [block_of(g2b, i * part) for i in range(blocks_up - half_up)],
        axis=1,
    )
    g3a, g3b = gather_group(third_piece, down_part // 2)
    reduce_full = jnp.concatenate([g3a, g3b], axis=2).reshape(ff, model_width)

    patch_ids = lax.axis_index("fsdp") * patch_count + jnp.arange(patch_count, dtype=jnp.int32)
    seq_ends = jnp.cumsum(seq_patches[0])
    seq_ids = jnp.sum((patch_ids[:, None] >= seq_ends[None, :]).astype(jnp.int32), axis=1)
    seq_hits = (seq_ids[:, None] == jnp.arange(seq_ends.shape[0], dtype=jnp.int32)[None, :]).astype(jnp.int32)
    end_of = jnp.sum(seq_hits * seq_ends[None, :], axis=1)
    fill_of = jnp.sum(seq_hits * last_fill[0][None, :], axis=1)
    in_patch = jnp.arange(PATCH, dtype=jnp.int32)
    keep_byte = (
        (patch_ids != end_of - 1)[:, None] | (in_patch[None, :] < fill_of[:, None])
    ).reshape(row_count, 1)

    residual_input = byte_input.astype(F32) + pick(arrived, send_place).astype(F32)
    attention_normed_input, attention_centered_scaled, attention_inverse_deviation = (
        apply_layer_normalize(residual_input, gain_full, shift_full)
    )
    first_in = attention_normed_input.astype(BF16)
    qkv_rows = jnp.dot(first_in, qkv_full, preferred_element_type=F32).astype(BF16)
    blocks = row_count // 128

    def heads_of(values, start):
        return lax.slice_in_dim(values, start, start + model_width, axis=1).reshape(
            blocks, 128, HEADS, HEAD_DIM
        )

    queries = heads_of(qkv_rows, 0)
    keys_part = heads_of(qkv_rows, model_width)
    values_part = heads_of(qkv_rows, 2 * model_width)
    allowed = block_mask(128)
    scores = attention_scores(queries, keys_part, allowed)
    top_score = jnp.max(scores, axis=3, keepdims=True)
    expo = jnp.exp(scores - top_score)
    total = jnp.sum(expo, axis=3, keepdims=True)
    log_total = top_score + jnp.log(total)
    probs = (expo / total).astype(BF16)
    mixed = jnp.einsum("ghqk,gkhd->gqhd", probs, values_part, preferred_element_type=F32)
    attended = mixed.reshape(row_count, model_width).astype(BF16)
    residual_midway = residual_input + jnp.dot(attended, outproj_full, preferred_element_type=F32)
    feedforward_normed_input, feedforward_centered_scaled, feedforward_inverse_deviation = (
        apply_layer_normalize(residual_midway, gain_later, shift_later)
    )
    second_in = feedforward_normed_input.astype(BF16)
    pre_act = jnp.dot(second_in, expand_full, preferred_element_type=F32) + expand_bias
    cumulative = 0.5 * (1.0 + jax.scipy.special.erf(pre_act * 0.7071067811865476))
    activ = (pre_act * cumulative).astype(BF16)
    result = residual_midway + jnp.dot(activ, reduce_full, preferred_element_type=F32) + reduce_bias
    layer_out = jnp.where(keep_byte, result, 0.0).astype(BF16)

    upstream_b = jnp.where(keep_byte, cotangent, jnp.zeros((), BF16))
    upstream = upstream_b.astype(F32)
    grad_reduce_bias = jnp.sum(upstream, axis=0)
    grad_reduce = contract_rows(activ, upstream_b)
    grad_activ = contract_cols(upstream_b, reduce_full)
    density = jnp.exp(-0.5 * jnp.square(pre_act)) * 0.3989422804014327
    grad_pre = (grad_activ * (cumulative + pre_act * density)).astype(BF16)
    grad_expand_bias = jnp.sum(grad_pre.astype(F32), axis=0)
    grad_expand = contract_rows(second_in, grad_pre)
    gradient_feedforward_branch = contract_cols(grad_pre, expand_full)
    normalize_piece, gradient_feedforward_gain, gradient_feedforward_shift = normalize_pullback(
        gradient_feedforward_branch,
        gain_later,
        feedforward_centered_scaled,
        feedforward_inverse_deviation,
    )
    grad_middle = upstream + normalize_piece
    grad_branch = grad_middle.astype(BF16)
    grad_outproj = contract_rows(attended, grad_branch)
    grad_attended = (
        contract_cols(grad_branch, outproj_full)
        .astype(BF16)
        .reshape(blocks, 128, HEADS, HEAD_DIM)
    )
    scores_again = attention_scores(queries, keys_part, allowed)
    probs_again = jnp.exp(scores_again - log_total)
    grad_probs = jnp.einsum(
        "gqhd,gkhd->ghqk", grad_attended, values_part, preferred_element_type=F32
    )
    grad_values = jnp.einsum(
        "ghqk,gqhd->gkhd", probs_again.astype(BF16), grad_attended, preferred_element_type=F32
    )
    grad_scores = (
        probs_again * (grad_probs - jnp.sum(probs_again * grad_probs, axis=3, keepdims=True))
    ).astype(BF16)
    grad_queries = jnp.einsum(
        "ghqk,gkhd->gqhd", grad_scores, keys_part, preferred_element_type=F32
    ) * HEAD_DIM ** (-0.5)
    grad_keys = jnp.einsum(
        "ghqk,gqhd->gkhd", grad_scores, queries, preferred_element_type=F32
    ) * HEAD_DIM ** (-0.5)
    grad_qkv = jnp.concatenate(
        [
            grad_queries.reshape(row_count, model_width),
            grad_keys.reshape(row_count, model_width),
            grad_values.reshape(row_count, model_width),
        ],
        axis=1,
    ).astype(BF16)
    gradient_attention_branch = contract_cols(grad_qkv, qkv_full)
    normalize_before_attention, gradient_attention_gain, gradient_attention_shift = (
        normalize_pullback(
            gradient_attention_branch,
            gain_full,
            attention_centered_scaled,
            attention_inverse_deviation,
        )
    )
    grad_input = (grad_middle + normalize_before_attention).astype(BF16)
    sent_back = lax.all_to_all(
        pick(grad_input, send_order), "fsdp", split_axis=0, concat_axis=0, tiled=True
    )
    inverse_slot = (
        jnp.zeros((patch_count,), jnp.int32)
        .at[wanted_slot]
        .set(jnp.arange(patch_count, dtype=jnp.int32))
    )
    grad_global = pick(sent_back, inverse_slot)
    grad_qkv_full = contract_rows(first_in, grad_qkv)

    red_a = links.core + links.x + links.y + links.z
    red_b = links.core + links.y + links.x + links.z

    def parts_of(values):
        return values.reshape(fsdp_count, split, values.shape[0] // (fsdp_count * split), -1)

    def owned(values, at):
        a = links.reduce(values[:, :, :at].astype(BF16), red_a)
        b = links.reduce(values[:, :, at:].astype(BF16), red_b)
        total = jnp.concatenate([a, b], axis=0)[None]
        steps = links.core + links.x
        total = links.gather(total, steps)
        quarters = jnp.arange(split, dtype=jnp.int32) ^ links.quarter
        place = jnp.zeros((split,), jnp.int32)
        for position, (_, mask) in enumerate(steps):
            place = place + ((quarters // mask) % 2) * (1 << position)
        return total[place].astype(F32)

    def column_blocks(values):
        return jnp.concatenate([parts_of(v) for v in cut(values)], axis=2)

    r3 = owned(parts_of(grad_reduce), down_part // 2)
    r2 = owned(column_blocks(grad_expand), half_up * part)
    vec_rows = jnp.concatenate(
        [
            v.reshape(fsdp_count, shard)
            for v in (
                gradient_attention_gain,
                gradient_attention_shift,
                gradient_feedforward_gain,
                gradient_feedforward_shift,
                grad_reduce_bias,
            )
        ],
        axis=1,
    )
    vec_rows = jnp.pad(vec_rows, ((0, 0), (0, model_width - vec_rows.shape[1])))
    bias_rows = grad_expand_bias.reshape(fsdp_count, -1)
    bias_rows = jnp.pad(bias_rows, ((0, 0), (0, model_width - bias_rows.shape[1])))
    vec_rows = jnp.pad(jnp.stack([vec_rows, bias_rows], axis=1), ((0, 0), (0, 6), (0, 0)))
    vec_rows = jnp.broadcast_to(vec_rows[:, None], (fsdp_count, split, 8, model_width))
    r1 = owned(
        jnp.concatenate([vec_rows, column_blocks(grad_qkv_full), parts_of(grad_outproj)], axis=2),
        8 + 2 * part,
    )

    def rows_of(values, start):
        return values[:, start : start + part].reshape(shard, model_width)

    own_vec = [r1[0, 0, i * shard : (i + 1) * shard] for i in range(5)]
    own_bias = r1[0, 1, : up_bias.shape[0]]
    return (
        layer_out,
        grad_input,
        grad_global,
        own_vec[0],
        own_vec[1],
        jnp.concatenate([rows_of(r1, 8 + i * part) for i in range(3)], axis=1),
        rows_of(r1, 8 + 3 * part),
        own_vec[2],
        own_vec[3],
        jnp.concatenate([rows_of(r2, i * part) for i in range(blocks_up)], axis=1),
        own_bias,
        r3.reshape(down_weight.shape[0], model_width),
        own_vec[4],
    )


def solution(mesh):
    in_specs = (
        P(("replica", "fsdp"), None),
        P(("replica", "fsdp"), None),
        P(("replica", "fsdp"), None),
        P("replica", None),
        P("replica", None),
        P("replica", "fsdp"),
        P("fsdp"),
        P("fsdp"),
        P("fsdp", None),
        P("fsdp", None),
        P("fsdp"),
        P("fsdp"),
        P("fsdp", None),
        P("fsdp"),
        P("fsdp", None),
        P("fsdp"),
    )
    out_specs = (
        P(("replica", "fsdp"), None),
        P(("replica", "fsdp"), None),
        P(("replica", "fsdp"), None),
        P("fsdp"),
        P("fsdp"),
        P("fsdp", None),
        P("fsdp", None),
        P("fsdp"),
        P("fsdp"),
        P("fsdp", None),
        P("fsdp"),
        P("fsdp", None),
        P("fsdp"),
    )
    return jax.shard_map(body, mesh=mesh, in_specs=in_specs, out_specs=out_specs, check_vma=False)
```
